32 devices in a mesh: grp: 8 (over y, x, core), dev: 4 (over z).
Axes of the slice: x: 2, y: 2, z: 4, core: 2. Of those that a mesh axis runs over, the one named last changes fastest.
Arguments:
- pixels: float32 [1024, 32, 768], P(('grp', 'dev')), may hold values from -6 to 6
- proj_weight: float32 [768, 1536], P('grp'), may hold values from -0.21875 to 0.21875
- gate_vector: float32 [1536], replicated, may hold values from -0.75 to 0.75
- slide_cot: float32 [128, 1536], P('grp'), may hold values from -6 to 6
- slide_owner: int32 [8, 16], P('grp'), may hold values from 0 to 3, as said below
- tile_slide: int32 [1024], P(('grp', 'dev')), may hold values from 0 to 15, as said below
- tile_count: int32 [32], P(('grp', 'dev')), may hold values from 16 to 32, as said below
Outputs:
- slide_embed: float32 [128, 1536], P(('grp', 'dev'))
- weight_grad: float32 [768, 1536], P('grp')
The draws below stay inside these ranges and needn't reach their ends.
Inputs may be any that keep to these rules, and one draw needn't show every extreme that they name: `slide_owner`: in each group every owner along dev owns exactly 4 slides. `tile_slide`: among the tissue tiles of one device, at most 8 belong to slides of one owner; in every group one owner receives exactly 8 from every device of the group. `tile_count`: slots below a device's count hold tissue; the rest are background and take no part. Some device of each group is full.
All inputs are finite; a program needn't handle non-finite values.
Results may differ from the reference program's by a relative error of at most 0.0001.
Values sent between devices are 32-bit elements; how exact they have to be, the bound alone decides.
No kernel may reach another device: no remote copies, remote signals or barrier semaphores. Data moves between devices by JAX's collectives and lax.ppermute only.
A program may use at most 64 MiB of HBM per device.

```python
import jax
import jax.numpy as jnp
from jax import lax

C = 768
F = 1536
P_SIZE = 32
TILES_DEV = 32
SLIDES_DEV = 4
CAP = 8
SLIDES = 128
TILES = 1024
N_GRP = 8
N_DEV = 4


def one_permutation(subkey):
    return jax.random.permutation(subkey, N_DEV * SLIDES_DEV).astype(jnp.int32)


def plan(key):
    keys = jax.random.split(jax.random.fold_in(key, 11), 7)
    perms = jax.vmap(one_permutation)(jax.random.split(keys[0], N_GRP))
    owners = (perms // SLIDES_DEV).astype(jnp.int32)
    inverse = jnp.argsort(perms, axis=1, stable=True).astype(jnp.int32)
    hottest = jax.random.randint(keys[1], (N_GRP, 1, 1), 0, N_DEV).astype(jnp.int32)
    counts = jax.random.randint(keys[2], (N_GRP, N_DEV), TILES_DEV // 2, TILES_DEV + 1).astype(jnp.int32)
    fullest = jax.random.randint(keys[3], (N_GRP, 1), 0, N_DEV).astype(jnp.int32)
    holder_ids = jnp.arange(N_DEV).astype(jnp.int32)[None, :]
    counts = jnp.where(holder_ids == fullest, TILES_DEV, jnp.where(holder_ids == (fullest + 1) % N_DEV, TILES_DEV // 2, counts)).astype(jnp.int32)
    scores = jax.random.randint(keys[4], (N_GRP, N_DEV, TILES_DEV), 0, 1 << 30).astype(jnp.int32)
    slot_ids = jnp.arange(TILES_DEV).astype(jnp.int32)
    tissue = slot_ids[None, None, :] < counts[:, :, None]
    earlier = scores[..., None, :]
    later = scores[..., :, None]
    before = (earlier < later) | (earlier == later) & (slot_ids[None, :] < slot_ids[:, None])
    ranks = jnp.sum((before & tissue[..., None, :]).astype(jnp.int32), axis=-1).astype(jnp.int32)
    shifts = jax.random.randint(keys[5], (N_GRP, N_DEV, 1), 0, N_DEV - 1).astype(jnp.int32)
    others = (hottest + 1 + (ranks - CAP + shifts) % (N_DEV - 1)) % N_DEV
    targets = jnp.where(ranks < CAP, hottest, others).astype(jnp.int32)
    picks = jax.random.randint(keys[6], (N_GRP, N_DEV, TILES_DEV), 0, SLIDES_DEV).astype(jnp.int32)
    wanted = (targets * SLIDES_DEV + picks).reshape(N_GRP, N_DEV * TILES_DEV).astype(jnp.int32)
    slides = jnp.take_along_axis(inverse, wanted, axis=1).reshape(-1).astype(jnp.int32)
    return (owners, slides, counts.reshape(-1))


def draw_slide_owner(key, part):
    return plan(key)[0]


def draw_tile_slide(key, part):
    return plan(key)[1]


def draw_tile_count(key, part):
    return plan(key)[2]


def raised(entries, rng, source, target, shards_of, factor):
    owner, partner = [(jnp.arange(entries.shape[position]) // (entries.shape[position] // shards_of)).reshape([-1 if axis == position else 1 for axis in range(entries.ndim)]) for position in (source, target)]
    chosen = jax.random.permutation(rng, shards_of)[partner]
    strong = (owner == chosen) | (owner == (partner + shards_of // 2) % shards_of)
    return jnp.where(strong, factor * entries, entries)


def steps_of(rng, extent, shards, low, high):
    def one(dim, blocks):
        draws = jax.random.uniform(jax.random.fold_in(jax.random.fold_in(rng, 6), dim), (blocks,), jnp.float32, low / len(shards), high / len(shards))
        return jnp.repeat(jnp.exp(draws), extent[dim] // blocks).reshape((-1,) + (1,) * (len(extent) - dim - 1))

    loudness = one(*shards[0])
    for cut in shards[1:]:
        loudness = loudness * one(*cut)
    return loudness


def centred(stream_key, shape, deviation, bound, shards=(), held_as=jnp.bfloat16):
    gain = steps_of(stream_key, shape, shards, -0.22, 0.18) if shards else 1.0
    entries = jax.random.normal(stream_key, shape, jnp.float32) * deviation * gain
    return jnp.minimum(jnp.maximum(entries, -bound), bound).astype(held_as)


def gaussian_with(rng, shape, scale, reach, shards, heavy, held_as=jnp.bfloat16):
    result = scale * jax.random.normal(rng, shape, jnp.float32)
    if shards:
        result = result * steps_of(rng, shape, shards, -0.22, 0.18)
    return jnp.clip(raised(result, jax.random.fold_in(rng, 3), *heavy), -reach, reach).astype(held_as)


def setup_inputs(seed: int = 0) -> dict:
    seeds = jax.random.split(jax.random.key(seed), 8)
    pixels = gaussian_with(seeds[0], (TILES, P_SIZE, C), 1.0, 6.0, ((0, 32),), (0, 2, 32, 2.75), jnp.float32)
    proj_weight = centred(seeds[1], (C, F), C ** -0.5, 0.21875, ((0, 8),), jnp.float32)
    gate_vector = centred(seeds[2], (F,), 64 ** -0.5, 0.75, (), jnp.float32)
    slide_cot = centred(seeds[3], (SLIDES, F), 1.0, 6.0, ((0, 8),), jnp.float32)
    slide_owner = draw_slide_owner(jax.random.fold_in(seeds[7], 71), 0)
    tile_slide = draw_tile_slide(jax.random.fold_in(seeds[7], 71), 0)
    tile_count = draw_tile_count(jax.random.fold_in(seeds[7], 71), 0)
    return {"pixels": pixels, "proj_weight": proj_weight, "gate_vector": gate_vector, "slide_cot": slide_cot, "slide_owner": slide_owner, "tile_slide": tile_slide, "tile_count": tile_count}


def reference(pixels, proj_weight, gate_vector, slide_cot, slide_owner, tile_slide, tile_count):
    exact = lax.Precision.HIGHEST
    devices = N_GRP * N_DEV
    group_slides = N_DEV * SLIDES_DEV
    blocks = pixels.reshape(devices, TILES_DEV, P_SIZE, C)

    def forward(block_in):
        hidden = jnp.dot(block_in.reshape(TILES_DEV * P_SIZE, C), proj_weight, precision=exact, preferred_element_type=jnp.float32)
        return jnp.mean((hidden * jax.nn.sigmoid(hidden)).reshape(TILES_DEV, P_SIZE, F), axis=1)

    tile_feat = lax.map(forward, blocks).reshape(TILES, F)
    tile_ids = jnp.arange(TILES).astype(jnp.int32)
    device_of = (tile_ids // TILES_DEV).astype(jnp.int32)
    slot_of = (tile_ids % TILES_DEV).astype(jnp.int32)
    tissue = (slot_of < tile_count[device_of]).astype(jnp.float32)
    slide_ids = ((device_of // N_DEV) * group_slides + tile_slide).astype(jnp.int32)
    gate = jax.nn.sigmoid(jnp.dot(tile_feat, gate_vector, precision=exact))
    sums = jax.ops.segment_sum((tissue * gate)[:, None] * tile_feat, slide_ids, num_segments=SLIDES)
    members = jax.ops.segment_sum(tissue, slide_ids, num_segments=SLIDES)
    divisor = jnp.maximum(members, 1.0)
    embed = sums / divisor[:, None]
    listing = jnp.argsort(slide_owner, axis=1, stable=True).astype(jnp.int32)
    listing = listing + (jnp.arange(N_GRP).astype(jnp.int32) * group_slides)[:, None]
    slide_embed = embed[listing.reshape(-1)]
    scaled = slide_cot[slide_ids] * (tissue / divisor[slide_ids])[:, None]
    inner_dot = jnp.sum(tile_feat * scaled, axis=1)
    tile_grad = gate[:, None] * scaled + (gate * (1.0 - gate) * inner_dot)[:, None] * gate_vector[None, :]
    grads = tile_grad.reshape(devices, TILES_DEV, F)

    def accumulate(total, item):
        block_in, grad_in = item
        flat = block_in.reshape(TILES_DEV * P_SIZE, C)
        hidden = jnp.dot(flat, proj_weight, precision=exact, preferred_element_type=jnp.float32)
        sigma = jax.nn.sigmoid(hidden)
        slope = (sigma * (1.0 + hidden * (1.0 - sigma))).reshape(TILES_DEV, P_SIZE, F)
        hidden_grad = ((grad_in / P_SIZE)[:, None, :] * slope).reshape(TILES_DEV * P_SIZE, F)
        term = lax.dot_general(flat, hidden_grad, (((0,), (0,)), ((), ())), precision=exact, preferred_element_type=jnp.float32)
        return total + term, None

    weight_grad, unused = lax.scan(accumulate, jnp.zeros((C, F), jnp.float32), (blocks, grads))
    return slide_embed, weight_grad
```

```python
import functools

import jax
import jax.numpy as jnp
from jax import lax
from jax.experimental import pallas as pl
from jax.experimental.pallas import tpu as pltpu
from jax.sharding import PartitionSpec as P

AXES = ("grp", "dev")
EXACT = lax.Precision.HIGHEST
BF16 = jnp.bfloat16
F32 = jnp.float32


def bits_of(n):
    return n.bit_length() - 1


def flip(value, nbits):
    return sum(((value >> i) & 1) << (nbits - 1 - i) for i in range(nbits))


def permute(value, n_grp, n_dev, move):
    pairs = []
    for g in range(n_grp):
        for z in range(n_dev):
            chip, core, row = move(g // 2, g % 2, z)
            pairs.append((g * n_dev + z, (chip * 2 + core) * n_dev + row))
    return lax.ppermute(value, AXES, pairs)


def split(value):
    high = value.astype(BF16)
    return high, (value - high.astype(F32)).astype(BF16)


def prep_kernel(x_ref, *refs):
    cat_ref, turned_ref = refs[-2:]
    width = x_ref.shape[1]
    high, low = split(x_ref[...])
    cat_ref[:, :width] = high
    cat_ref[:, width:] = low
    turned_ref[0] = high.T
    turned_ref[1] = low.T


def prep(rows, held, second, block):
    count, width = rows.shape
    steps = count // block
    start = steps if second else 0
    outs = (
        jax.ShapeDtypeStruct((2 * count, 2 * width), BF16),
        jax.ShapeDtypeStruct((2, width, 2 * count), BF16),
    )
    return pl.pallas_call(
        prep_kernel,
        grid=(steps,),
        out_shape=outs,
        in_specs=[pl.BlockSpec((block, width), lambda i: (i, 0))]
        + [pl.BlockSpec(memory_space=pl.ANY)] * len(held),
        out_specs=(
            pl.BlockSpec((block, 2 * width), lambda i: (i + start, 0)),
            pl.BlockSpec((2, width, block), lambda i: (0, 0, i + start)),
        ),
        input_output_aliases={1: 0, 2: 1} if held else {},
        cost_estimate=pl.CostEstimate(
            flops=4 * count * width, bytes_accessed=12 * count * width, transcendentals=0
        ),
        name="prep_second" if second else "prep_first",
    )(rows, *held)


def forward_kernel(positions, order_ref, x_ref, *refs):
    w_refs, (slope_ref, feat_ref, w_high, w_low) = refs[:-4], refs[-4:]
    width = w_high.shape[0]
    unit = w_refs[0].shape[0]

    @pl.when(pl.program_id(0) == 0)
    def _():
        place = 0
        for w_ref in w_refs:
            for part in range(w_ref.shape[0] // unit):
                high, low = split(w_ref[part * unit : (part + 1) * unit, :])
                rows = pl.ds(pl.multiple_of(order_ref[place] * unit, unit), unit)
                w_high[rows, :] = high
                w_low[rows, :] = low
                place += 1

    dot = functools.partial(jnp.dot, preferred_element_type=F32)
    hidden = (
        dot(x_ref[:, :width], w_high[...])
        + dot(x_ref[:, width:], w_high[...])
        + dot(x_ref[:, :width], w_low[...])
    )
    sigma = jax.nn.sigmoid(hidden)
    act = hidden * sigma
    slope_ref[...] = sigma + act * (1.0 - sigma)
    tiles = x_ref.shape[0] // positions
    feat_ref[...] = jnp.sum(act.reshape(tiles, positions, act.shape[1]), axis=1) * (1.0 / positions)


def forward(cat, w_parts, order, positions, block):
    count, width = cat.shape[0], cat.shape[1] // 2
    columns = w_parts[0].shape[1]
    grid_spec = pltpu.PrefetchScalarGridSpec(
        num_scalar_prefetch=1,
        grid=(count // block,),
        in_specs=[pl.BlockSpec((block, 2 * width), lambda i, o: (i, 0))]
        + [pl.BlockSpec(w.shape, lambda i, o: (0, 0)) for w in w_parts],
        out_specs=(
            pl.BlockSpec((block, columns), lambda i, o: (i, 0)),
            pl.BlockSpec((block // positions, columns), lambda i, o: (i, 0)),
        ),
        scratch_shapes=[pltpu.VMEM((width, columns), BF16)] * 2,
    )
    return pl.pallas_call(
        functools.partial(forward_kernel, positions),
        grid_spec=grid_spec,
        out_shape=(
            jax.ShapeDtypeStruct((count, columns), F32),
            jax.ShapeDtypeStruct((count // positions, columns), F32),
        ),
        cost_estimate=pl.CostEstimate(
            flops=6 * count * width * columns,
            bytes_accessed=4 * count * (width + columns),
            transcendentals=count * columns,
        ),
        name="forward",
    )(order, cat, *w_parts)


def backward_kernel(positions, halves, order_ref, slope_ref, grad_ref, turned_ref, *refs):
    send_ref, keep_ref, g_high, g_low = refs
    step = pl.program_id(0)

    @pl.when(step == 0)
    def _():
        count, columns = slope_ref.shape
        tiles = count // positions
        spread = slope_ref[...].reshape(tiles, positions, columns) * grad_ref[...][:, None, :]
        high, low = split(spread.reshape(count, columns))
        g_high[...] = high
        g_low[...] = low

    dot = functools.partial(jnp.dot, preferred_element_type=F32)
    part = (
        dot(turned_ref[0], g_high[...])
        + dot(turned_ref[1], g_high[...])
        + dot(turned_ref[0], g_low[...])
    )

    @pl.when(step < halves)
    def _():
        send_ref[...] = part

    @pl.when(step >= halves)
    def _():
        keep_ref[...] = part


def backward(slope, grad, turned, order, positions):
    count, columns = slope.shape
    width = turned.shape[1]
    chips = order.shape[0]
    unit = width // chips
    halves = chips // 2
    grid_spec = pltpu.PrefetchScalarGridSpec(
        num_scalar_prefetch=1,
        grid=(chips,),
        in_specs=[
            pl.BlockSpec((count, columns), lambda i, o: (0, 0)),
            pl.BlockSpec(grad.shape, lambda i, o: (0, 0)),
            pl.BlockSpec((2, unit, count), lambda i, o: (0, o[(i + halves) % chips], 0)),
        ],
        out_specs=(
            pl.BlockSpec((unit, columns), lambda i, o: (jnp.minimum(i, halves - 1), 0)),
            pl.BlockSpec((unit, columns), lambda i, o: (jnp.maximum(i - halves, 0), 0)),
        ),
        scratch_shapes=[pltpu.VMEM((count, columns), BF16)] * 2,
    )
    half = jax.ShapeDtypeStruct((halves * unit, columns), F32)
    return pl.pallas_call(
        functools.partial(backward_kernel, positions, halves),
        grid_spec=grid_spec,
        out_shape=(half, half),
        cost_estimate=pl.CostEstimate(
            flops=6 * count * width * columns,
            bytes_accessed=4 * count * (width + columns),
            transcendentals=0,
        ),
        name="backward",
    )(order, slope, grad, turned)


def local(pixels, proj_weight, gate_vector, slide_cot, slide_owner, tile_slide, tile_count):
    n_grp, n_dev = lax.axis_size("grp"), lax.axis_size("dev")
    num_tiles, positions, width_in = pixels.shape
    rows_dev, width_out = proj_weight.shape
    chips, half = n_grp // 2, width_out // 2
    chip_bits, dev_bits = bits_of(chips), bits_of(n_dev)
    group = lax.axis_index("grp")
    chip, core, row = group // 2, group % 2, lax.axis_index("dev")
    first = core == 0
    move = functools.partial(permute, n_grp=n_grp, n_dev=n_dev)

    def swap(value):
        return move(value, move=lambda q, c, z: (q, 1 - c, z))

    def cross(value, step):
        return move(
            value,
            move=lambda q, c, z: (q ^ (1 << (step if c == 0 else chip_bits - 1 - step)), c, z),
        )

    def along(value, bit):
        return move(value, move=lambda q, c, z: (q, c, z ^ (1 << bit)))

    def shift(value, by):
        return move(value, move=lambda q, c, z: (q, c, (z + by) % n_dev))

    def mine(value):
        return jnp.where(first, value[:, :half], value[:, half:])

    def theirs(value):
        return jnp.where(first, value[:, half:], value[:, :half])

    plain = jnp.arange(chips, dtype=jnp.int32)
    turned_bits = jnp.array([flip(r, chip_bits) for r in range(chips)], jnp.int32)
    order = jnp.bitwise_xor(chip.astype(jnp.int32), jnp.where(first, plain, turned_bits))

    own_w = mine(proj_weight)
    other_w = swap(theirs(proj_weight))
    pix_rows = pixels.reshape(num_tiles * positions, width_in)
    pix_other = swap(pix_rows)

    owners = slide_owner[0]
    group_slides = owners.shape[0]
    slides_dev = group_slides // n_dev
    is_tissue = jnp.arange(num_tiles) < tile_count[0]
    slide_ids = jnp.arange(group_slides)
    member_hot = (
        (tile_slide[:, None] == slide_ids[None, :]) & is_tissue[:, None]
    ).astype(F32)
    counts = jnp.sum(member_hot, axis=0)[None, :]
    totals = counts
    for by in range(1, n_dev):
        totals = totals + shift(counts, by)
    divisor = jnp.maximum(totals[0], 1.0)
    before = (owners[None, :] < owners[:, None]) | (
        (owners[None, :] == owners[:, None]) & (slide_ids[None, :] < slide_ids[:, None])
    )
    rank = jnp.sum(before.astype(jnp.int32), axis=1)
    share = member_hot / divisor[None, :]
    listed = jnp.dot(
        share, (rank[:, None] == slide_ids[None, :]).astype(F32), precision=EXACT
    )
    cot_tiles = jnp.dot(share, slide_cot, precision=EXACT)
    message = jnp.concatenate([theirs(cot_tiles), listed], axis=1)
    arrived = swap(message)
    cot_both = jnp.concatenate([mine(cot_tiles), arrived[:, :half]], axis=0)
    listed_both = (listed, arrived[:, half:])

    block = 256
    held = prep(pix_rows, (), False, block)
    cat, turned = prep(pix_other, held, True, block)

    chip_w = jnp.concatenate(
        [jnp.where(first, own_w, other_w), jnp.where(first, other_w, own_w)], axis=0
    )
    columns = 256
    cuts = [slice(at, at + columns) for at in range(0, half, columns)]
    slopes, feats = [], []
    for cut in cuts:
        parts = [chip_w[:, cut]]
        for step in range(chip_bits):
            sent = parts[0] if step == 0 else jnp.concatenate(parts, axis=0)
            parts.append(cross(sent, step))
        slope, feat = forward(cat, parts, order, positions, 512)
        slopes.append(slope)
        feats.append(feat)
    feat = jnp.concatenate(feats, axis=1)

    gate_half = jnp.where(first, gate_vector[:half], gate_vector[half:])
    sums = jnp.stack(
        [jnp.sum(feat * gate_half[None, :], axis=1), jnp.sum(feat * cot_both, axis=1)], axis=0
    )
    sums_other = swap(sums)
    sums_other = jnp.concatenate([sums_other[:, num_tiles:], sums_other[:, :num_tiles]], axis=1)
    sums = sums + sums_other
    gate = jax.nn.sigmoid(sums[0])
    inner = gate * (1.0 - gate) * sums[1]
    tile_grad = (
        gate[:, None] * cot_both + inner[:, None] * gate_half[None, :]
    ) * (1.0 / positions)

    done = []
    for at, cut in enumerate(cuts):
        send, keep = backward(slopes[at], tile_grad[:, cut], turned, order, positions)
        for step in reversed(range(chip_bits)):
            got = cross(send, step)
            part = keep.shape[0] // 2
            if step:
                send = keep[part:] + got[part:]
                keep = keep[:part] + got[:part]
            else:
                keep = keep + got
        low, high = keep[:rows_dev], keep[rows_dev:]
        got = swap(jnp.where(first, high, low))
        kept = jnp.where(first, low, high)
        both = jnp.concatenate(
            [jnp.where(first, kept, got), jnp.where(first, got, kept)], axis=1
        )
        for bit in range(dev_bits - 1):
            low, high = jnp.split(both, 2, axis=0)
            even = (row >> bit) & 1 == 0
            both = jnp.where(even, low, high) + along(jnp.where(even, high, low), bit)
        if dev_bits:
            both = both + along(both, dev_bits - 1)
        for bit in reversed(range(dev_bits - 1)):
            got = along(both, bit)
            even = (row >> bit) & 1 == 0
            both = jnp.concatenate(
                [jnp.where(even, both, got), jnp.where(even, got, both)], axis=0
            )
        done.append(both)
    weight_grad = jnp.concatenate(
        [part[:, :columns] for part in done] + [part[:, columns:] for part in done], axis=1
    )

    weighted = gate[:, None] * feat
    pooled = jnp.stack(
        [
            lax.dot_general(
                listed_both[part],
                weighted[part * num_tiles : (part + 1) * num_tiles],
                (((0,), (0,)), ((), ())),
                precision=EXACT,
            ).reshape(n_dev, slides_dev, half)
            for part in (0, 1)
        ],
        axis=1,
    )
    embed = lax.dynamic_index_in_dim(pooled, row, 0, keepdims=False)
    for by in range(1, n_dev):
        embed = embed + shift(
            lax.dynamic_index_in_dim(pooled, (row + by) % n_dev, 0, keepdims=False), by
        )
    other = swap(embed[1])
    slide_embed = jnp.concatenate(
        [jnp.where(first, embed[0], other), jnp.where(first, other, embed[0])], axis=1
    )
    return (slide_embed, weight_grad)


def solution(mesh):
    return jax.shard_map(
        local,
        mesh=mesh,
        in_specs=(
            P(("grp", "dev"), None, None),
            P("grp", None),
            P(),
            P("grp", None),
            P("grp", None),
            P(("grp", "dev")),
            P(("grp", "dev")),
        ),
        out_specs=(P(("grp", "dev"), None), P("grp", None)),
        check_vma=False,
    )
```

```python
import functools

import jax
import jax.numpy as jnp
from jax import lax
from jax.experimental import pallas as pl
from jax.experimental.pallas import tpu as pltpu
from jax.sharding import PartitionSpec as P

AXES = ("grp", "dev")
EXACT = lax.Precision.HIGHEST
BF16 = jnp.bfloat16
F32 = jnp.float32
I32 = jnp.int32
VMEM = pl.BlockSpec(memory_space=pltpu.VMEM)
SMEM = pl.BlockSpec(memory_space=pltpu.SMEM)
ANY = pl.BlockSpec(memory_space=pl.ANY)
MIB = 1 << 20


def bits_of(n):
    return n.bit_length() - 1


def split(value):
    high = value.astype(BF16)
    return high, (value - high.astype(F32)).astype(BF16)


def dot(left, right):
    return jnp.dot(left, right, preferred_element_type=F32)


def place():
    group = lax.axis_index("grp").astype(I32)
    return group >> 1, group & 1, lax.axis_index("dev").astype(I32)


def span(index, size):
    return pl.ds(pl.multiple_of(index * size, size), size)


def whole(value):
    return pl.BlockSpec(value.shape, lambda *_: (0,) * value.ndim)


def call(kernel, name, outs, limit=8, flops=0, moved=0, **more):
    return pl.pallas_call(
        kernel,
        out_shape=tuple(jax.ShapeDtypeStruct(shape, dtype) for shape, dtype in outs),
        compiler_params=pltpu.CompilerParams(vmem_limit_bytes=limit * MIB),
        cost_estimate=pl.CostEstimate(flops=flops, bytes_accessed=moved, transcendentals=0),
        name=name,
        **more,
    )


def prep(rows, name, weight=None, block=256):
    count, width = rows.shape

    def kernel(x_ref, *refs):
        if weight is not None:
            weight_ref, mine_ref = refs[0], refs[-1]
            refs = refs[1:3]

            @pl.when(pl.program_id(0) == 0)
            def _():
                mine_ref[...] = weight_ref[:, span(place()[1], mine_ref.shape[1])]

        cat_ref, turned_ref = refs
        at = span(pl.program_id(0), block)
        high, low = split(x_ref[...])
        cat_ref[at, :width] = high
        cat_ref[at, width:] = low
        turned_ref[0, :, at] = high.T
        turned_ref[1, :, at] = low.T

    more = () if weight is None else (weight,)
    return call(
        kernel,
        name,
        [((count, 2 * width), BF16), ((2, width, count), BF16)]
        + [((w.shape[0], w.shape[1] // 2), F32) for w in more],
        grid=(count // block,),
        in_specs=[pl.BlockSpec((block, width), lambda i: (i, 0))] + [whole(w) for w in more],
        out_specs=(VMEM,) * (2 + len(more)),
        moved=12 * count * width,
    )(rows, *more)


def pack(mine, other):
    rows, half = mine.shape

    def kernel(mine_ref, other_ref, chip_ref, part_ref):
        _, core, row = place()
        own = mine_ref[...]
        theirs = other_ref[:, span(core, half)]
        chip_ref[span(core, rows), :] = own
        chip_ref[span(1 - core, rows), :] = theirs
        part_ref[...] = jnp.where(core == (row & 1), own, theirs)

    return call(
        kernel,
        "pack",
        [((2 * rows, half), F32), ((rows, half), F32)],
        in_specs=[VMEM, VMEM],
        out_specs=(VMEM, VMEM),
        moved=24 * rows * half,
    )(mine, other)


def count(tile_slide, tile_count, slides):
    def kernel(number_ref, slide_ref, out_ref):
        tiles = slide_ref.shape[1]
        hot = lax.broadcasted_iota(I32, (slides, tiles), 0) == slide_ref[...]
        hot = hot & (lax.broadcasted_iota(I32, (slides, tiles), 1) < number_ref[0])
        total = jnp.sum(hot.astype(F32), axis=1, keepdims=True)
        out_ref[...] = jnp.broadcast_to(total, out_ref.shape)

    return call(
        kernel,
        "count",
        [((slides, 128), F32)],
        in_specs=[SMEM, whole(tile_slide)],
        out_specs=(VMEM,),
    )(tile_count, tile_slide)[0]


def share(tile_slide, tile_count, owners, cot, totals):
    tiles = tile_slide.shape[1]
    slides, width = cot.shape
    half = width // 2

    def kernel(number_ref, slide_ref, owner_ref, cot_ref, total_ref, mine_ref, send_ref):
        _, core, row = place()
        hot = lax.broadcasted_iota(I32, (slides, tiles), 0) == slide_ref[...]
        hot = hot & (lax.broadcasted_iota(I32, (slides, tiles), 1) < number_ref[0])
        divisor = jnp.maximum(total_ref[:, :1], 1.0)
        shares = hot.astype(F32) / divisor
        square = (slides, slides)
        down, along = (lax.broadcasted_iota(I32, square, axis) for axis in (0, 1))
        owner = owner_ref[...] ^ row
        wide = jnp.broadcast_to(owner, square)
        tall = jnp.sum(jnp.where(down == along, wide, 0), axis=1, keepdims=True)
        before = (tall < wide) | ((tall == wide) & (down < along))
        rank = jnp.sum(before.astype(F32), axis=0, keepdims=True)
        listing = (down.astype(F32) == rank).astype(F32)
        listed = jnp.dot(listing, shares, precision=EXACT, preferred_element_type=F32)
        tile_cot = lax.dot_general(
            shares,
            cot_ref[...],
            (((0,), (0,)), ((), ())),
            precision=EXACT,
            preferred_element_type=F32,
        )
        low, high = tile_cot[:, :half], tile_cot[:, half:]
        mine_ref[:tiles, :] = jnp.where(core == 0, low, high)
        send_ref[:tiles, :] = jnp.where(core == 0, high, low)
        mine_ref[tiles:, :] = jnp.zeros((slides, half), F32)
        send_ref[tiles:, :] = jnp.zeros((slides, half), F32)
        mine_ref[tiles:, :tiles] = listed
        send_ref[tiles:, :tiles] = listed

    return call(
        kernel,
        "share",
        [((tiles + slides, half), F32)] * 2,
        in_specs=[SMEM, whole(tile_slide), whole(owners), whole(cot), VMEM],
        out_specs=(VMEM, VMEM),
        moved=8 * (tiles + slides) * width,
    )(tile_count, tile_slide, owners, cot, totals)


def forward(cat_a, cat_b, parts, spots, gate_vector, mine, theirs, positions, block=512):
    count, width = cat_a.shape[0], cat_a.shape[1] // 2
    half = parts[0].shape[1]
    tiles_dev = count // positions
    steps = count // block
    tiles = block // positions

    def kernel(a_ref, b_ref, *refs):
        w_refs = refs[: len(parts)]
        gate_ref, mine_ref, theirs_ref = refs[len(parts) : len(parts) + 3]
        slope_ref, feat_ref, sums_ref, w_high, w_low = refs[len(parts) + 3 :]
        step = pl.program_id(0)
        chip, core, row = place()

        @pl.when(step == 0)
        def _():
            for w_ref, spot in zip(w_refs, spots(chip, row)):
                high, low = split(w_ref[...])
                unit = width // lax.axis_size("grp")
                rows = pl.ds(pl.multiple_of(spot * unit, unit), w_ref.shape[0])
                w_high[rows, :] = high
                w_low[rows, :] = low

        def go(x_ref, at):
            rows = span(at, block)
            x_high, x_low = x_ref[rows, :width], x_ref[rows, width:]
            hidden = dot(x_high, w_high[...]) + dot(x_low, w_high[...]) + dot(x_high, w_low[...])
            sigma = jax.nn.sigmoid(hidden)
            act = hidden * sigma
            slope_ref[span(step, block), :] = sigma + act * (1.0 - sigma)
            feat_ref[span(step, tiles), :] = jnp.sum(
                act.reshape(tiles, positions, half), axis=1
            ) * (1.0 / positions)

        @pl.when(step < steps)
        def _():
            go(a_ref, step)

        @pl.when(step >= steps)
        def _():
            go(b_ref, step - steps)

        @pl.when(step == 2 * steps - 1)
        def _():
            gate = gate_ref[:, span(core, half)]
            for part, cot_ref in ((0, mine_ref), (1, theirs_ref)):
                rows = slice(part * tiles_dev, (part + 1) * tiles_dev)
                feat = feat_ref[rows, :]
                lane = lax.broadcasted_iota(I32, (tiles_dev, 128), 1)
                first = jnp.sum(feat * gate, axis=1, keepdims=True)
                second = jnp.sum(feat * cot_ref[:tiles_dev, :], axis=1, keepdims=True)
                sums_ref[rows, :] = jnp.where(lane == 0, first, second)

    return call(
        kernel,
        "forward",
        [((2 * count, half), F32), ((2 * tiles_dev, half), F32), ((2 * tiles_dev, 128), F32)],
        limit=16,
        grid=(2 * steps,),
        in_specs=[VMEM] * (2 + len(parts)) + [whole(gate_vector), VMEM, VMEM],
        out_specs=(VMEM,) * 3,
        scratch_shapes=[pltpu.VMEM((width, half), BF16)] * 2,
        flops=12 * count * width * half,
        moved=8 * count * half,
    )(cat_a, cat_b, *parts, gate_vector, mine, theirs)


def both_sums(own_ref, other_ref):
    tiles = own_ref.shape[0] // 2
    total = own_ref[...] + jnp.concatenate([other_ref[tiles:, :], other_ref[:tiles, :]], axis=0)
    gate = jax.nn.sigmoid(total[:, :1])
    return gate, gate * (1.0 - gate) * total[:, 1:2]


def backward(slope, turned, own, other, gate_vector, mine, theirs, positions, chips, cut):
    turned_a, turned_b = turned
    half = slope.shape[1]
    columns = cut.stop - cut.start
    width, count = turned_a.shape[1:]
    tiles = count // positions
    unit = width // chips
    far = [r for r in range(1, chips) if r & (r - 1)]
    near = [r for r in range(1, chips) if not r & (r - 1)]

    def kernel(slope_ref, a_ref, b_ref, own_ref, other_ref, gate_ref, mine_ref, theirs_ref, *refs):
        far_refs = refs[: 2 * len(far)]
        near_refs = refs[2 * len(far) : -3]
        keep_ref, g_high, g_low = refs[-3:]
        chip, core, row = place()
        gate, inner = both_sums(own_ref, other_ref)
        spot = pl.ds(pl.multiple_of(core * half + cut.start, 128), columns)
        vector = gate_ref[:, spot]
        for part, cot_ref in ((0, mine_ref), (1, theirs_ref)):
            some = slice(part * tiles, (part + 1) * tiles)
            rows = slice(part * count, (part + 1) * count)
            grad = (gate[some] * cot_ref[:tiles, cut] + inner[some] * vector) * (1.0 / positions)
            spread = slope_ref[rows, cut].reshape(tiles, positions, columns) * grad[:, None, :]
            high, low = split(spread.reshape(count, columns))
            g_high[rows, :] = high
            g_low[rows, :] = low

        def block(r):
            rows = span(chip ^ r, unit)
            out = None
            for part, x_ref in ((0, a_ref), (1, b_ref)):
                some = slice(part * count, (part + 1) * count)
                high = x_ref[0, rows, :]
                term = (
                    dot(high, g_high[some, :])
                    + dot(x_ref[1, rows, :], g_high[some, :])
                    + dot(high, g_low[some, :])
                )
                out = term if out is None else out + term
            return out

        for at, r in enumerate(far):
            value = block(r)
            even = (row & 1) == 0
            low, high = value[: unit // 2], value[unit // 2 :]
            far_refs[2 * at][...] = jnp.where(even, high, low)
            far_refs[2 * at + 1][...] = jnp.where(even, low, high)
        for ref, r in zip(near_refs, near):
            ref[...] = block(r)
        keep_ref[...] = block(0)

    outs = [((unit // 2, columns), F32)] * (2 * len(far)) + [((unit, columns), F32)] * (
        len(near) + 1
    )
    results = call(
        kernel,
        "backward",
        outs,
        limit=16,
        in_specs=[VMEM] * 5 + [whole(gate_vector), VMEM, VMEM],
        out_specs=(VMEM,) * len(outs),
        scratch_shapes=[pltpu.VMEM((2 * count, columns), BF16)] * 2,
        flops=12 * count * width * columns,
        moved=8 * count * columns,
    )(slope, turned_a, turned_b, own, other, gate_vector, mine, theirs)
    send, hold = results[0 : 2 * len(far) : 2], results[1 : 2 * len(far) : 2]
    return far, send, hold, near, results[2 * len(far) : -1], results[-1]


def merge(keep, near, far):
    rows, columns = keep.shape
    size = rows // 2

    def kernel(*refs):
        near_refs, far_refs = refs[: 1 + len(near)], refs[1 + len(near) : -2]
        send_ref, keep_ref = refs[-2:]
        parity = place()[2] & 1
        first, second = span(parity, size), span(1 - parity, size)
        total = sum(ref[first, :] for ref in near_refs)
        keep_ref[...] = total + sum(ref[...] for ref in far_refs)
        send_ref[...] = sum(ref[second, :] for ref in near_refs)

    return call(
        kernel,
        "merge",
        [((size, columns), F32)] * 2,
        in_specs=[VMEM] * (1 + len(near) + len(far)),
        out_specs=(VMEM, VMEM),
        moved=4 * rows * columns * (2 + len(near)),
    )(keep, *near, *far)


def pool(feat, own, other, mine, theirs, tiles, slides):
    half = feat.shape[1]

    def kernel(feat_ref, own_ref, other_ref, mine_ref, theirs_ref, keep_ref, send_ref):
        gate, _ = both_sums(own_ref, other_ref)
        for part, cot_ref, out_ref in ((0, mine_ref, keep_ref), (1, theirs_ref, send_ref)):
            rows = slice(part * tiles, (part + 1) * tiles)
            out_ref[...] = jnp.dot(
                cot_ref[tiles:, :tiles],
                gate[rows] * feat_ref[rows, :],
                precision=EXACT,
                preferred_element_type=F32,
            )

    return call(
        kernel,
        "pool",
        [((slides, half), F32)] * 2,
        in_specs=[VMEM] * 5,
        out_specs=(VMEM, VMEM),
        moved=8 * slides * half,
    )(feat, own, other, mine, theirs)


def join(own, other):
    rows, half = own.shape

    def kernel(own_ref, other_ref, out_ref):
        core = place()[1]
        out_ref[:, span(core, half)] = own_ref[...]
        out_ref[:, span(1 - core, half)] = other_ref[...]

    return call(
        kernel,
        "join",
        [((rows, 2 * half), F32)],
        in_specs=[VMEM, VMEM],
        out_specs=(VMEM,),
        moved=16 * rows * half,
    )(own, other)[0]


def finish(joined, arrived):
    rows = joined[0].shape[0]
    sizes = [part.shape[1] // 2 for part in joined]
    half = sum(sizes)

    def kernel(*refs):
        own_refs, got_refs, out_ref = refs[: len(sizes)], refs[len(sizes) : -1], refs[-1]
        _, core, row = place()
        held = core == (row & 1)
        start = 0
        for own_ref, got_ref, size in zip(own_refs, got_refs, sizes):
            part = jnp.where(held, own_ref[...], got_ref[...])
            out_ref[:, start : start + size] = part[:, :size]
            out_ref[:, half + start : half + start + size] = part[:, size:]
            start += size

    return call(
        kernel,
        "finish",
        [((rows, 2 * half), F32)],
        in_specs=[VMEM] * (2 * len(sizes)),
        moved=24 * rows * half,
    )(*joined, *arrived)[0]


def local(pixels, proj_weight, gate_vector, slide_cot, slide_owner, tile_slide, tile_count):
    n_grp, n_dev = lax.axis_size("grp"), lax.axis_size("dev")
    num_tiles, positions, width_in = pixels.shape
    rows_dev, width_out = proj_weight.shape
    chips, half = n_grp // 2, width_out // 2
    dev_bits = bits_of(n_dev)
    slides = slide_cot.shape[0]

    def permute(value, move):
        pairs = []
        for g in range(n_grp):
            for z in range(n_dev):
                target = move(g // 2, g % 2, z)
                if target is not None:
                    to_chip, to_core, to_row = target
                    pairs.append((g * n_dev + z, (to_chip * 2 + to_core) * n_dev + to_row))
        return lax.ppermute(value, AXES, pairs)

    def swap(value):
        return permute(value, lambda q, c, z: (q, 1 - c, z))

    def cross(value, r):
        return permute(value, lambda q, c, z: (q ^ r, c, z))

    def along(value, bit):
        return permute(value, lambda q, c, z: (q, c, z ^ (1 << bit)))

    other_w = swap(proj_weight)
    pix_rows = pixels.reshape(num_tiles * positions, width_in)
    pix_sent, other_w = lax.optimization_barrier((pix_rows, other_w))
    pix_other = swap(pix_sent)
    cat_a, turned_a, mine_w = prep(pix_rows, "prep_own", proj_weight)

    near = [r for r in range(1, chips) if not r & (r - 1)]
    far = [r for r in range(1, chips) if r & (r - 1)]
    chip_w, half_w = pack(mine_w, other_w)
    cat_b, turned_b = prep(pix_other, "prep_other")
    far_parts = [cross(half_w, r) for r in far]
    *far_parts, cat_b = lax.optimization_barrier((*far_parts, cat_b))
    near_parts = [cross(chip_w, r) for r in near]
    far_others = [along(part, 0) for part in far_parts]
    parts = [chip_w, *near_parts, *far_parts, *far_others]

    def spots(at_chip, at_row):
        odd = at_row & 1
        return (
            [2 * at_chip]
            + [2 * (at_chip ^ r) for r in near]
            + [2 * (at_chip ^ r) + odd for r in far]
            + [2 * (at_chip ^ r) + 1 - odd for r in far]
        )

    slide_row = tile_slide[None, :]
    totals = count(slide_row, tile_count, slides)
    for bit in range(dev_bits):
        totals = totals + along(totals, bit)
    mine, send = share(slide_row, tile_count, slide_owner, slide_cot, totals)
    theirs = swap(send)
    gate_row = gate_vector[None, :]

    slope, feat, own = forward(
        cat_a, cat_b, parts, spots, gate_row, mine, theirs, positions
    )
    other = swap(own)

    cuts = [slice(0, 2 * half // 3), slice(2 * half // 3, half)]
    joined, arrived = [], []
    for cut in cuts:
        _, sent, held, _, near_blocks, keep = backward(
            slope, (turned_a, turned_b), own, other, gate_row, mine, theirs, positions, chips, cut
        )
        paired = [along(part, 0) for part in sent]
        near_got = [cross(part, r) for part, r in zip(near_blocks, near)]
        far_got = [cross(part + got, r) for part, got, r in zip(held, paired, far)]
        sent, kept = merge(keep, near_got, far_got)
        kept = kept + along(sent, 0)
        for bit in range(1, dev_bits):
            kept = kept + along(kept, bit)
        got = permute(kept, lambda q, c, z: (q, 1 - c, z) if c != z % 2 else None)
        joined.append(join(kept, got))
        arrived.append(
            permute(joined[-1], lambda q, c, z: (q, c, z ^ 1) if c == z % 2 else None)
        )
    weight_grad = finish(joined, arrived)

    keep, send = pool(feat, own, other, mine, theirs, num_tiles, slides)
    got = swap(send)
    embed = join(keep, got)
    for bit in reversed(range(dev_bits)):
        size = embed.shape[0] // 2
        embed = embed[:size] + along(embed[size:], bit)
    return (embed, weight_grad)


def solution(mesh):
    return jax.shard_map(
        local,
        mesh=mesh,
        in_specs=(
            P(("grp", "dev"), None, None),
            P("grp", None),
            P(),
            P("grp", None),
            P("grp", None),
            P(("grp", "dev")),
            P(("grp", "dev")),
        ),
        out_specs=(P(("grp", "dev"), None), P("grp", None)),
        check_vma=False,
    )
```
